32 devices in a mesh: dp: 16 (over z, x, core), tensor: 2 (over y).
Axes of the slice: x: 2, y: 2, z: 4, core: 2. Of those that a mesh axis runs over, the one named last changes fastest.
Arguments:
- tokens: bfloat16 [320, 6144], P('dp', 'tensor'), may hold values from -6 to 6
- route_ids: int32 [320, 2], replicated, may hold values from 0 to 3, all different within a row
- route_probs: bfloat16 [320, 2], replicated, may hold values from 0.099609375 to 1
- w_gate: bfloat16 [4, 6144, 8192], P(None, 'tensor', 'dp'), may hold values from -0.078125 to 0.078125
- w_up: bfloat16 [4, 6144, 8192], P(None, 'tensor', 'dp'), may hold values from -0.078125 to 0.078125
- w_down: bfloat16 [4, 8192, 6144], P(None, 'dp', 'tensor'), may hold values from -0.0625 to 0.0625
Outputs:
- mixed_out: bfloat16 [320, 6144], P('dp', 'tensor')
The draws below stay inside these ranges and needn't reach their ends.
Inputs may be any that keep to these rules, and one draw needn't show every extreme that they name: `route_ids`: each row names 2 different experts, and every expert is named by some row.
All inputs are finite; a program needn't handle non-finite values.
Results may differ from the reference program's by a relative error of at most 0.0049.
Values may be sent and summed in bfloat16 or wider, within the bound.
No kernel may reach another device: no remote copies, remote signals or barrier semaphores. Data moves between devices by JAX's collectives and lax.ppermute only.
A program may use at most 128 MiB of HBM per device.

```python
import jax
import jax.numpy as jnp
from jax import lax

D = 6144
FF = 8192
EXPERTS = 4
TOPK = 2
TOKENS = 320


def block_levels(own_key, extent, split, low, high):
    factor_of, own = 1.0, jax.random.fold_in(own_key, 6)
    for dim, shards_of in split:
        draws = jnp.exp(jax.random.uniform(jax.random.fold_in(own, dim), (shards_of,), jnp.float32, low / len(split), high / len(split)))
        factor_of = factor_of * jnp.repeat(draws, extent[dim] // shards_of).reshape([-1 if axis == dim else 1 for axis in range(len(extent))])
    return factor_of


def different_ones(stream_key, rows, number_of, top, lift):
    order = jax.random.permutation(jax.random.fold_in(stream_key, 1), number_of)
    favour = order
    for power in range(3):
        favour = favour * favour // number_of
    favour = favour * lift // number_of
    chance = jax.random.randint(jax.random.fold_in(stream_key, 2), (rows, number_of), 0, 4096) + favour
    fixed_rows = jax.random.permutation(jax.random.fold_in(stream_key, 3), rows)[jnp.arange(number_of) % rows]
    chance = jnp.where(jnp.arange(rows)[:, None] == fixed_rows[None, :], 1 << 14, chance)
    score = chance * number_of + jnp.arange(number_of)
    return lax.top_k(score.astype(jnp.int32), top)[1].astype(jnp.int32)


def noise(key, shape, width, most, split=(), kind=jnp.bfloat16):
    values = jax.random.normal(key, shape, jnp.float32) * width
    if len(split) > 0:
        values = block_levels(key, shape, split, -0.22, 0.18) * values
    return jnp.clip(values, min=-most, max=most).astype(kind)


def setup_inputs(seed: int = 0) -> dict:
    keys = jax.random.split(jax.random.key(seed), 7)
    tokens = noise(keys[0], (TOKENS, D), 1.0, 6.0, ((0, 16), (1, 2)))
    route_ids = different_ones(keys[1], TOKENS, EXPERTS, TOPK, 8192)
    route_probs = jnp.clip(jax.random.uniform(keys[2], (TOKENS, TOPK), jnp.float32, 0.099609375, 1.0), 0.099609375, 1.0).astype(jnp.bfloat16)
    w_gate = noise(keys[3], (EXPERTS, D, FF), D ** -0.5, 0.078125, ((1, 2), (2, 16)))
    w_up = noise(keys[4], (EXPERTS, D, FF), D ** -0.5, 0.078125, ((1, 2), (2, 16)))
    w_down = noise(keys[5], (EXPERTS, FF, D), FF ** -0.5, 0.0625, ((1, 16), (2, 2)))
    return dict(tokens=tokens, route_ids=route_ids, route_probs=route_probs, w_gate=w_gate, w_up=w_up, w_down=w_down)


def reference(tokens, route_ids, route_probs, w_gate, w_up, w_down):
    route_weight = route_probs.astype(jnp.float32)
    mixed_sum = jnp.zeros((TOKENS, D), jnp.float32)
    for expert in range(EXPERTS):
        chosen = jnp.sum(jnp.where(route_ids == expert, route_weight, 0.0), axis=1)
        gate_sum = jnp.dot(tokens, w_gate[expert], preferred_element_type=jnp.float32)
        up_sum = jnp.dot(tokens, w_up[expert], preferred_element_type=jnp.float32)
        hidden = (gate_sum * jax.nn.sigmoid(gate_sum) * up_sum).astype(jnp.bfloat16)
        expert_out = jnp.dot(hidden, w_down[expert], preferred_element_type=jnp.float32)
        mixed_sum = mixed_sum + chosen[:, None] * expert_out
    return mixed_sum.astype(jnp.bfloat16)
```

```python
import functools

import jax
import jax.numpy as jnp
from jax import lax
from jax.experimental import pallas as pl
from jax.experimental.pallas import tpu as pltpu
from jax.sharding import PartitionSpec as P

BF = jnp.bfloat16
F32 = jnp.float32


def tile_of(width, most):
    tile = min(width, most)
    while width % tile:
        tile //= 2
    return tile


def up_kernel(n, where_ref, ids_ref, own_ref, other_ref, wg_ref, wu_ref, keep_ref, send_ref, acc_ref):
    e = pl.program_id(1)
    half, me = where_ref[0], where_ref[1]
    top = ids_ref.shape[1]
    rows = keep_ref.shape[2]
    for which, w_ref in enumerate((wg_ref, wu_ref)):
        part = jnp.dot(own_ref[...], w_ref[0, half], preferred_element_type=F32)
        part += jnp.dot(other_ref[...], w_ref[0, 1 - half], preferred_element_type=F32)
        for k in range(top):
            chosen = ids_ref[:, k : k + 1] == e
            acc_ref[which, k] = jnp.where(chosen, part, acc_ref[which, k])

    @pl.when(e == pl.num_programs(1) - 1)
    def _():
        for s in range(n):
            begin = pl.multiple_of(lax.rem(me + s, n) * rows, rows)
            block = acc_ref[:, :, pl.ds(begin, rows), :]
            if s == 0:
                keep_ref[...] = block
            else:
                send_ref[s - 1] = block.astype(BF)


def up_gemm(n, where, ids, own, other, w_gate, w_up):
    token_count, top = ids.shape
    experts, width, hidden = w_gate.shape
    half = own.shape[1]
    tile = tile_of(hidden, 256)
    rows = token_count // n
    weight = pl.BlockSpec((1, 2, half, tile), lambda j, e, w: (e, 0, 0, j))
    tokens = pl.BlockSpec((token_count, half), lambda j, e, w: (0, 0))
    return pl.pallas_call(
        functools.partial(up_kernel, n),
        grid_spec=pltpu.PrefetchScalarGridSpec(
            num_scalar_prefetch=1,
            grid=(hidden // tile, experts),
            in_specs=[
                pl.BlockSpec((token_count, top), lambda j, e, w: (0, 0)),
                tokens,
                tokens,
                weight,
                weight,
            ],
            out_specs=[
                pl.BlockSpec((2, top, rows, tile), lambda j, e, w: (0, 0, 0, j)),
                pl.BlockSpec((n - 1, 2, top, rows, tile), lambda j, e, w: (0, 0, 0, 0, j)),
            ],
            scratch_shapes=[pltpu.VMEM((2, top, token_count, tile), F32)],
        ),
        out_shape=[
            jax.ShapeDtypeStruct((2, top, rows, hidden), F32),
            jax.ShapeDtypeStruct((n - 1, 2, top, rows, hidden), BF),
        ],
        cost_estimate=pl.CostEstimate(
            flops=4 * token_count * width * hidden * experts,
            bytes_accessed=4 * experts * width * hidden,
            transcendentals=0,
        ),
        name="up_gemm",
    )(where, ids, own, other, w_gate.reshape(experts, 2, half, hidden), w_up.reshape(experts, 2, half, hidden))


def down_kernel(n, where_ref, ids_ref, probs_ref, *refs):
    hidden_refs, (wd_ref, out_ref, rows_ref) = refs[:n], refs[n:]
    me = where_ref[1]
    experts = wd_ref.shape[0]
    top, rows = hidden_refs[0].shape[:2]

    @pl.when(pl.program_id(0) == 0)
    def _():
        for s in range(n):
            begin = pl.multiple_of(lax.rem(me + n - s, n) * rows, rows)
            for e in range(experts):
                total = jnp.zeros(hidden_refs[s].shape[1:], F32)
                for k in range(top):
                    chosen = ids_ref[pl.ds(begin, rows), k : k + 1] == e
                    total = jnp.where(chosen, hidden_refs[s][k].astype(F32), total)
                rows_ref[e, pl.ds(begin, rows), :] = total.astype(BF)

    mixed = None
    for e in range(experts):
        share = jnp.zeros((ids_ref.shape[0], 1), F32)
        for k in range(top):
            share = jnp.where(ids_ref[:, k : k + 1] == e, probs_ref[:, k : k + 1], share)
        term = share * jnp.dot(rows_ref[e], wd_ref[e], preferred_element_type=F32)
        mixed = term if mixed is None else mixed + term
    out_ref[...] = mixed.astype(out_ref.dtype)


def down_gemm(n, where, ids, probs, hiddens, w_down, own, dtype):
    token_count, top = ids.shape
    experts, hidden, width = w_down.shape
    half = width // 2
    tile = tile_of(half, 512)
    tiles = half // tile
    rows = token_count // n
    small = pl.BlockSpec((token_count, top), lambda j, w: (0, 0))

    def column(j, w):
        side = w[0] if own else 1 - w[0]
        return (0, 0, side * tiles + j)

    return pl.pallas_call(
        functools.partial(down_kernel, n),
        grid_spec=pltpu.PrefetchScalarGridSpec(
            num_scalar_prefetch=1,
            grid=(tiles,),
            in_specs=[small, small]
            + [pl.BlockSpec((top, rows, hidden), lambda j, w: (0, 0, 0))] * n
            + [pl.BlockSpec((experts, hidden, tile), column)],
            out_specs=pl.BlockSpec((token_count, tile), lambda j, w: (0, j)),
            scratch_shapes=[pltpu.VMEM((experts, token_count, hidden), BF)],
        ),
        out_shape=jax.ShapeDtypeStruct((token_count, half), dtype),
        cost_estimate=pl.CostEstimate(
            flops=2 * token_count * half * hidden * experts,
            bytes_accessed=2 * experts * half * hidden,
            transcendentals=0,
        ),
        name="down_own" if own else "down_other",
    )(where, ids, probs, *hiddens, w_down)


def local(tokens, route_ids, route_probs, w_gate, w_up, w_down):
    members = lax.axis_size("dp")
    n = lax.axis_size("tensor")
    chips = members // 2
    swap = [(i, i ^ 1) for i in range(members)]
    planes = [[2 * i + c for i in range(chips)] for c in range(2)]
    side = lax.axis_index("dp") % 2
    me = lax.axis_index("tensor")
    where = jnp.stack([side, me]).astype(jnp.int32)
    local_rows, width = tokens.shape
    half = width // 2
    first = side == 0
    probs = route_probs.astype(F32)

    def on_chip(x):
        return lax.ppermute(x, "dp", swap)

    def pair(mine, theirs, axis):
        return jnp.concatenate(
            [jnp.where(first, mine, theirs), jnp.where(first, theirs, mine)], axis=axis
        )

    left, right = tokens[:, :half], tokens[:, half:]
    theirs = on_chip(jnp.where(first, right, left))
    block = pair(jnp.where(first, left, right), theirs, 0)
    own = lax.all_to_all(
        jnp.broadcast_to(block[None], (chips,) + block.shape), "dp", 0, 0, tiled=True, axis_index_groups=planes
    ).reshape(chips * 2 * local_rows, half)
    other = on_chip(own)

    keep, send = up_gemm(n, where, route_ids, own, other, w_gate, w_up)
    sums = keep
    for s in range(1, n):
        shift = [(i, (i + s) % n) for i in range(n)]
        sums = sums + lax.ppermute(send[s - 1], "tensor", shift).astype(F32)
    gate_sum, up_sum = sums[0], sums[1]
    hidden = (gate_sum * jax.nn.sigmoid(gate_sum) * up_sum).astype(BF)
    hiddens = [hidden]
    for s in range(1, n):
        shift = [(i, (i + s) % n) for i in range(n)]
        hiddens.append(lax.ppermute(hidden, "tensor", shift))

    away = on_chip(down_gemm(n, where, route_ids, probs, hiddens, w_down, False, BF))
    stay = down_gemm(n, where, route_ids, probs, hiddens, w_down, True, F32)
    parts = (stay + away.astype(F32)).astype(BF).reshape(chips, 2 * local_rows, half)
    terms = lax.all_to_all(parts, "dp", 0, 0, tiled=True, axis_index_groups=planes)
    mixed = jnp.sum(terms.astype(F32), axis=0).astype(BF)
    top, bottom = mixed[:local_rows], mixed[local_rows:]
    others = on_chip(jnp.where(first, bottom, top))
    return pair(jnp.where(first, top, bottom), others, 1)


def solution(mesh):
    placed = (
        P("dp", "tensor"),
        P(),
        P(),
        P(None, "tensor", "dp"),
        P(None, "tensor", "dp"),
        P(None, "dp", "tensor"),
    )
    return jax.shard_map(
        local, mesh=mesh, in_specs=placed, out_specs=P("dp", "tensor"), check_vma=False
    )
```

```python
import functools

import jax
import jax.numpy as jnp
from jax import lax
from jax.experimental import pallas as pl
from jax.experimental.pallas import tpu as pltpu
from jax.sharding import PartitionSpec as P

BF = jnp.bfloat16
F32 = jnp.float32
LIMIT = 10 * 1024 * 1024


def tile_of(width, most):
    tile = min(width, most)
    while width % tile:
        tile //= 2
    return tile


def fetch_kernel(source_ref, target_ref, sem_ref):
    copies = [
        pltpu.make_async_copy(source_ref.at[e], target_ref.at[e], sem_ref.at[e]) for e in range(source_ref.shape[0])
    ]
    for copy in copies:
        copy.start()
    for copy in copies:
        copy.wait()


def fetch(w):
    return pl.pallas_call(
        fetch_kernel,
        in_specs=[pl.BlockSpec(memory_space=pltpu.HBM)],
        out_specs=pl.BlockSpec(memory_space=pltpu.VMEM),
        out_shape=pltpu.VMEM(w.shape, w.dtype),
        scratch_shapes=[pltpu.SemaphoreType.DMA((w.shape[0],))],
        cost_estimate=pl.CostEstimate(flops=0, bytes_accessed=4 * w.size, transcendentals=0),
        compiler_params=pltpu.CompilerParams(vmem_limit_bytes=LIMIT),
        name="fetch",
    )(pltpu.with_memory_space_constraint(w, pltpu.HBM))


def up_kernel(n, part, where_ref, ids_ref, own_ref, other_ref, wg_ref, wu_ref, keep_ref, send_ref, acc_ref):
    half, me = where_ref[0], where_ref[1]
    experts = wg_ref.shape[0]
    top = ids_ref.shape[1]
    rows, tile = keep_ref.shape[2:]
    columns = pl.ds(part * tile, tile)
    for e in range(experts):
        for which, w_ref in enumerate((wg_ref, wu_ref)):
            block = jnp.dot(own_ref[...], w_ref[e, half, :, columns], preferred_element_type=F32)
            block += jnp.dot(other_ref[...], w_ref[e, 1 - half, :, columns], preferred_element_type=F32)
            for k in range(top):
                if e > 0:
                    chosen = ids_ref[:, k : k + 1] == e
                    acc_ref[which, k] = jnp.where(chosen, block, acc_ref[which, k])
                else:
                    acc_ref[which, k] = block
    for s in range(n):
        begin = pl.multiple_of(lax.rem(me + s, n) * rows, rows)
        block = acc_ref[:, :, pl.ds(begin, rows), :]
        if s == 0:
            keep_ref[...] = block
        else:
            send_ref[s - 1] = block.astype(BF)


def up_gemm(n, part, parts, where, ids, own, other, w_gate, w_up):
    token_count, top = ids.shape
    experts, unused, half, hidden = w_gate.shape
    rows = token_count // n
    tile = hidden // parts
    inside = pl.BlockSpec(memory_space=pltpu.VMEM)
    return pl.pallas_call(
        functools.partial(up_kernel, n, part),
        in_specs=[pl.BlockSpec(memory_space=pltpu.SMEM)] + [inside] * 5,
        out_specs=[inside] * 2,
        scratch_shapes=[pltpu.VMEM((2, top, token_count, tile), F32)],
        out_shape=[
            jax.ShapeDtypeStruct((2, top, rows, tile), F32),
            jax.ShapeDtypeStruct((n - 1, 2, top, rows, tile), BF),
        ],
        cost_estimate=pl.CostEstimate(
            flops=8 * token_count * half * tile * experts,
            bytes_accessed=8 * experts * half * tile,
            transcendentals=0,
        ),
        compiler_params=pltpu.CompilerParams(vmem_limit_bytes=LIMIT),
        name="up_gemm",
    )(where, ids, own, other, w_gate, w_up)


def down_kernel(n, parts, own, where_ref, ids_ref, probs_ref, *refs):
    hidden_refs, (wd_ref, out_ref, rows_ref, acc_ref) = refs[: n * parts], refs[n * parts :]
    me = where_ref[1]
    side = where_ref[0] if own else 1 - where_ref[0]
    experts, hidden, width = wd_ref.shape
    half = width // 2
    top, rows, depth = hidden_refs[0].shape
    tile = tile_of(half, 512)
    for e in range(experts):
        for s in range(n):
            begin = pl.multiple_of(lax.rem(me + n - s, n) * rows, rows)
            for part in range(parts):
                source_ref = hidden_refs[part * n + s]
                total = jnp.zeros((rows, depth), F32)
                for k in range(top):
                    chosen = ids_ref[pl.ds(begin, rows), k : k + 1] == e
                    total = jnp.where(chosen, source_ref[k].astype(F32), total)
                rows_ref[e, pl.ds(begin, rows), part * depth : (part + 1) * depth] = total.astype(BF)
        share = jnp.zeros((ids_ref.shape[0], 1), F32)
        for k in range(top):
            share = jnp.where(ids_ref[:, k : k + 1] == e, probs_ref[:, k : k + 1], share)
        for j in range(half // tile):
            columns = pl.ds(j * tile, tile)
            source = pl.ds(pl.multiple_of(side * half + j * tile, tile), tile)
            term = share * jnp.dot(rows_ref[e], wd_ref[e, :, source], preferred_element_type=F32)
            if e > 0:
                term += acc_ref[:, columns]
            if e < experts - 1:
                acc_ref[:, columns] = term
            else:
                out_ref[:, columns] = term


def down_gemm(n, parts, where, ids, probs, hiddens, w_down, own):
    token_count, top = ids.shape
    experts, hidden, width = w_down.shape
    half = width // 2
    inside = pl.BlockSpec(memory_space=pltpu.VMEM)
    return pl.pallas_call(
        functools.partial(down_kernel, n, parts, own),
        in_specs=[pl.BlockSpec(memory_space=pltpu.SMEM)] + [inside] * (3 + n * parts),
        out_specs=inside,
        scratch_shapes=[
            pltpu.VMEM((experts, token_count, hidden), BF),
            pltpu.VMEM((token_count, half), F32),
        ],
        out_shape=jax.ShapeDtypeStruct((token_count, half), F32),
        cost_estimate=pl.CostEstimate(
            flops=2 * token_count * half * hidden * experts,
            bytes_accessed=2 * experts * half * hidden,
            transcendentals=0,
        ),
        compiler_params=pltpu.CompilerParams(vmem_limit_bytes=LIMIT),
        name="down_own" if own else "down_other",
    )(where, ids, probs, *hiddens, w_down)


def local(tokens, route_ids, route_probs, w_gate, w_up, w_down):
    members = lax.axis_size("dp")
    n = lax.axis_size("tensor")
    lines = members // 4
    place = lax.axis_index("dp")
    side = place % 2
    me = lax.axis_index("tensor")
    where = jnp.stack([side, me]).astype(jnp.int32)
    local_rows, width = tokens.shape
    half = width // 2
    first = side == 0
    experts, unused, hidden_width = w_gate.shape
    top = route_ids.shape[1]
    w_gate = w_gate.reshape(experts, 2, half, hidden_width)
    w_up = w_up.reshape(experts, 2, half, hidden_width)
    chip_rows = 2 * local_rows
    parts = 2 if hidden_width % 256 == 0 else 1
    cut = half // 128 * 2 // 3 * 128

    def flip(x, bits):
        return lax.ppermute(x, "dp", [(i, i ^ bits) for i in range(members)])

    def on_chip(x):
        return flip(x, 1)

    def over_x(x):
        return flip(x, 2)

    def over_z(x, k):
        return flip(x, 4 * k)

    def over_tensor(x, s):
        return lax.ppermute(x, "tensor", [(i, (i + s) % n) for i in range(n)])

    def pair(mine, theirs, axis):
        return jnp.concatenate(
            [jnp.where(first, mine, theirs), jnp.where(first, theirs, mine)], axis=axis
        )

    def in_order(x):
        chips = jnp.stack([(place // 2) ^ (2 * k + xr) for xr in range(2) for k in range(lines)])
        return x.reshape(2 * lines, chip_rows * top)[chips].reshape(2 * lines * chip_rows, top)

    ids, probs = in_order(route_ids), in_order(route_probs.astype(F32))

    left, right = tokens[:, :half], tokens[:, half:]
    theirs = on_chip(jnp.where(first, right, left))
    block = pair(jnp.where(first, left, right), theirs, 0)
    near, far = block[:, :cut], block[:, cut:]
    near, far, w_gate, ids, probs, where = lax.optimization_barrier((near, far, w_gate, ids, probs, where))
    w_gate = fetch(w_gate)
    near_line = [near] + [over_z(near, k) for k in range(1, lines)]
    far_pair = [far, over_x(far)]
    near_all = jnp.concatenate(near_line, axis=0)
    far_both = jnp.concatenate(far_pair, axis=0)
    near_all, far_both, w_gate, w_up = lax.optimization_barrier((near_all, far_both, w_gate, w_up))
    w_up = fetch(w_up)
    near_other = over_x(near_all)
    far_line = [far_both] + [over_z(far_both, k) for k in range(1, lines)]
    near_other, far_line, w_up = lax.optimization_barrier((near_other, far_line, w_up))
    far_all = [jnp.concatenate([f[xr * chip_rows : (xr + 1) * chip_rows] for f in far_line], axis=0) for xr in range(2)]
    own = jnp.concatenate(
        [jnp.concatenate([near_all, near_other], axis=0), jnp.concatenate(far_all, axis=0)], axis=1
    )
    other = on_chip(own)

    hiddens = []
    for part in range(parts):
        keep, send = up_gemm(n, part, parts, where, ids, own, other, w_gate, w_up)
        if part == parts - 1:
            send, w_down = lax.optimization_barrier((send, w_down))
            w_down = fetch(w_down)
        sums = keep
        for s in range(1, n):
            sums = sums + over_tensor(send[s - 1], s).astype(F32)
        gate_sum, up_sum = sums[0], sums[1]
        hidden = (gate_sum * jax.nn.sigmoid(gate_sum) * up_sum).astype(BF)
        hiddens += [hidden] + [over_tensor(hidden, s) for s in range(1, n)]

    away = on_chip(down_gemm(n, parts, where, ids, probs, hiddens, w_down, False))
    stay = down_gemm(n, parts, where, ids, probs, hiddens, w_down, True)
    total = (stay + away).reshape(2, lines, chip_rows, half)
    sent = total.astype(BF)
    near_x = over_x(sent[1, :, :, :cut])
    far_z = [over_z(sent[:, k, :, cut:], k) for k in range(1, lines)]
    near_sum = total[0, :, :, :cut] + near_x.astype(F32)
    far_sum = total[:, 0, :, cut:]
    for part in far_z:
        far_sum = far_sum + part.astype(F32)
    near_z = [over_z(near_sum[k].astype(BF), k) for k in range(1, lines)]
    far_x = over_x(far_sum[1].astype(BF))
    near_sum = near_sum[0]
    for part in near_z:
        near_sum = near_sum + part.astype(F32)
    far_sum = far_sum[0] + far_x.astype(F32)
    mixed = jnp.concatenate([near_sum, far_sum], axis=1).astype(BF)
    upper, lower = mixed[:local_rows], mixed[local_rows:]
    others = on_chip(jnp.where(first, lower, upper))
    return pair(jnp.where(first, upper, lower), others, 1)


def solution(mesh):
    placed = (
        P("dp", "tensor"),
        P(),
        P(),
        P(None, "tensor", "dp"),
        P(None, "tensor", "dp"),
        P(None, "dp", "tensor"),
    )
    return jax.shard_map(
        local, mesh=mesh, in_specs=placed, out_specs=P("dp", "tensor"), check_vma=False
    )
```

```python
import functools

import jax
import jax.numpy as jnp
from jax import lax
from jax.experimental import pallas as pl
from jax.experimental.pallas import tpu as pltpu
from jax.sharding import PartitionSpec as P


BF = jnp.bfloat16
F32 = jnp.float32
LIMIT = 10 * 1024 * 1024


def tile_of(width, most):
    tile = min(width, most)
    while width % tile:
        tile //= 2
    return tile


def copies_of(source, target, sem):
    count, depth = target.shape[0], target.shape[1] // 2
    copies = []
    for e in range(count):
        for part in range(2):
            piece = pl.ds(part * depth, depth)
            copies.append(pltpu.make_async_copy(source(e).at[piece], target.at[e, piece], sem.at[e, part]))
    return copies


def fetch_kernel(part, source_ref, target_ref, sem_ref):
    copies = copies_of(lambda e: source_ref.at[e, part], target_ref, sem_ref)
    for copy in copies:
        copy.start()
    for copy in copies:
        copy.wait()


def in_hbm(w):
    return pltpu.with_memory_space_constraint(w, pltpu.HBM)


def fetch(w, part):
    shape = w.shape[:1] + w.shape[2:]
    return pl.pallas_call(
        functools.partial(fetch_kernel, part),
        in_specs=[pl.BlockSpec(memory_space=pltpu.HBM)],
        out_specs=pl.BlockSpec(memory_space=pltpu.VMEM),
        out_shape=pltpu.VMEM(shape, w.dtype),
        scratch_shapes=[pltpu.SemaphoreType.DMA((w.shape[0], 2))],
        cost_estimate=pl.CostEstimate(flops=0, bytes_accessed=4 * w.size // w.shape[1], transcendentals=0),
        compiler_params=pltpu.CompilerParams(vmem_limit_bytes=LIMIT),
        name="fetch",
    )(in_hbm(w))


def order_kernel(lines, chip_rows, where_ref, ids_ref, probs_ref, wu_ref, ids_out, probs_out, fetched_ref, sem_ref):
    copies = copies_of(lambda e: wu_ref.at[e], fetched_ref, sem_ref)
    for copy in copies:
        copy.start()
    top, token_count = ids_ref.shape
    row = lax.broadcasted_iota(jnp.int32, (chip_rows, token_count), 0)
    column = lax.broadcasted_iota(jnp.int32, (chip_rows, token_count), 1)
    for i, (xr, k) in enumerate((xr, k) for xr in range(2) for k in range(lines)):
        source = jnp.bitwise_xor(where_ref[2], 2 * k + xr) * chip_rows
        mine = column == row + source
        rows = slice(i * chip_rows, (i + 1) * chip_rows)
        for k in range(top):
            ids = jnp.where(mine, ids_ref[k : k + 1, :].astype(F32), 0.0)
            probs = jnp.where(mine, probs_ref[k : k + 1, :].astype(F32), 0.0)
            ids_out[rows, k : k + 1] = jnp.sum(ids, axis=1, keepdims=True).astype(jnp.int32)
            probs_out[rows, k : k + 1] = jnp.sum(probs, axis=1, keepdims=True)
    for copy in copies:
        copy.wait()


def order(lines, chip_rows, where, ids, probs, w_up):
    count = w_up.shape[0] - w_up.shape[0] // 2
    token_count, top = ids.shape
    inside = pl.BlockSpec(memory_space=pltpu.VMEM)
    return pl.pallas_call(
        functools.partial(order_kernel, lines, chip_rows),
        in_specs=[pl.BlockSpec(memory_space=pltpu.SMEM), inside, inside, pl.BlockSpec(memory_space=pltpu.HBM)],
        out_specs=[inside] * 3,
        out_shape=[
            jax.ShapeDtypeStruct((token_count, top), jnp.int32),
            jax.ShapeDtypeStruct((token_count, top), F32),
            pltpu.VMEM((count,) + w_up.shape[1:], w_up.dtype),
        ],
        scratch_shapes=[pltpu.SemaphoreType.DMA((count, 2))],
        cost_estimate=pl.CostEstimate(flops=0, bytes_accessed=4 * w_up.size // 2, transcendentals=0),
        compiler_params=pltpu.CompilerParams(vmem_limit_bytes=LIMIT),
        name="order",
    )(where, ids.T, probs.T, in_hbm(w_up))


def share_out(n, me, acc_ref, keep_ref, send_ref):
    rows = keep_ref.shape[1]
    for s in range(n):
        begin = pl.multiple_of(lax.rem(me + s, n) * rows, rows)
        block = acc_ref[:, pl.ds(begin, rows), :]
        if s == 0:
            keep_ref[...] = block
        else:
            send_ref[s - 1] = block.astype(BF)


def gate_kernel(n, stage, where_ref, ids_ref, rows_ref, wg_ref, *refs):
    copies = []
    if stage == 0:
        wu_ref, acc_ref, fetched_ref, sem_ref = refs
        last = wu_ref.shape[0] - fetched_ref.shape[0]
        copies = copies_of(lambda e: wu_ref.at[last + e], fetched_ref, sem_ref)
    else:
        base_ref, keep_ref, send_ref, acc_ref = refs
    for copy in copies:
        copy.start()
    half = where_ref[0] if stage == 0 else 1 - where_ref[0]
    tile = tile_of(wg_ref.shape[3], 256)
    for e in range(wg_ref.shape[0]):
        for j in range(wg_ref.shape[3] // tile):
            columns = pl.ds(j * tile, tile)
            block = jnp.dot(rows_ref[...], wg_ref[e, half, :, columns], preferred_element_type=F32)
            for k in range(acc_ref.shape[0]):
                value = block if stage == 0 else block + base_ref[k, :, columns]
                if e > 0:
                    value = jnp.where(ids_ref[:, k : k + 1] == e, value, acc_ref[k, :, columns])
                acc_ref[k, :, columns] = value
    if stage == 1:
        share_out(n, where_ref[1], acc_ref, keep_ref, send_ref)
    for copy in copies:
        copy.wait()


def gate_gemm(n, stage, where, ids, rows, w_gate, extra):
    token_count, top = ids.shape
    experts, _, half, hidden = w_gate.shape
    inside = pl.BlockSpec(memory_space=pltpu.VMEM)
    outside = pl.BlockSpec(memory_space=pltpu.HBM)
    whole = (top, token_count, hidden)
    count = experts // 2
    if stage == 0:
        extra, extra_spec = in_hbm(extra), outside
        out_shape = [jax.ShapeDtypeStruct(whole, F32), pltpu.VMEM((count, 2, half, hidden), BF)]
        scratch = [pltpu.SemaphoreType.DMA((count, 2))]
    else:
        extra_spec = inside
        out_shape = [
            jax.ShapeDtypeStruct((top, token_count // n, hidden), F32),
            jax.ShapeDtypeStruct((n - 1, top, token_count // n, hidden), BF),
        ]
        scratch = [pltpu.VMEM(whole, F32)]
    return pl.pallas_call(
        functools.partial(gate_kernel, n, stage),
        in_specs=[pl.BlockSpec(memory_space=pltpu.SMEM)] + [inside] * 3 + [extra_spec],
        out_specs=[inside] * len(out_shape),
        scratch_shapes=scratch,
        out_shape=out_shape,
        cost_estimate=pl.CostEstimate(
            flops=2 * token_count * half * hidden * experts,
            bytes_accessed=2 * experts * half * hidden,
            transcendentals=0,
        ),
        compiler_params=pltpu.CompilerParams(vmem_limit_bytes=LIMIT),
        name="gate_gemm",
    )(where, ids, rows, w_gate, extra)


def up_kernel(n, part, where_ref, ids_ref, own_ref, other_ref, *refs):
    weight_refs, (keep_ref, send_ref, acc_ref) = refs[:-3], refs[-3:]
    half = where_ref[0]
    tile = acc_ref.shape[2]
    columns = pl.ds(part * tile, tile)
    e = 0
    for w_ref in weight_refs:
        for i in range(w_ref.shape[0]):
            block = jnp.dot(own_ref[...], w_ref[i, half, :, columns], preferred_element_type=F32)
            block += jnp.dot(other_ref[...], w_ref[i, 1 - half, :, columns], preferred_element_type=F32)
            for k in range(acc_ref.shape[0]):
                value = block
                if e > 0:
                    value = jnp.where(ids_ref[:, k : k + 1] == e, value, acc_ref[k])
                acc_ref[k] = value
            e += 1
    share_out(n, where_ref[1], acc_ref, keep_ref, send_ref)


def up_gemm(n, part, parts, where, ids, own, other, weights):
    token_count, top = ids.shape
    half, hidden = weights[0].shape[2:]
    experts = sum(w.shape[0] for w in weights)
    rows = token_count // n
    tile = hidden // parts
    inside = pl.BlockSpec(memory_space=pltpu.VMEM)
    return pl.pallas_call(
        functools.partial(up_kernel, n, part),
        in_specs=[pl.BlockSpec(memory_space=pltpu.SMEM)] + [inside] * (3 + len(weights)),
        out_specs=[inside] * 2,
        scratch_shapes=[pltpu.VMEM((top, token_count, tile), F32)],
        out_shape=[
            jax.ShapeDtypeStruct((top, rows, tile), F32),
            jax.ShapeDtypeStruct((n - 1, top, rows, tile), BF),
        ],
        cost_estimate=pl.CostEstimate(
            flops=4 * token_count * half * tile * experts,
            bytes_accessed=4 * experts * half * tile,
            transcendentals=0,
        ),
        compiler_params=pltpu.CompilerParams(vmem_limit_bytes=LIMIT),
        name="up_gemm",
    )(where, ids, own, other, *weights)


def pick_rows(n, me, ids_ref, hidden_refs, rows_ref):
    top, rows, depth = hidden_refs[0].shape
    for s in range(n):
        begin = pl.multiple_of(lax.rem(me + n - s, n) * rows, rows)
        for e in range(rows_ref.shape[0]):
            total = jnp.zeros((rows, depth), F32)
            for k in range(top):
                chosen = ids_ref[pl.ds(begin, rows), k : k + 1] == e
                total = jnp.where(chosen, hidden_refs[s][k].astype(F32), total)
            rows_ref[e, pl.ds(begin, rows), :] = total.astype(BF)


def share_of(ids_ref, probs_ref, e):
    share = jnp.zeros((ids_ref.shape[0], 1), F32)
    for k in range(ids_ref.shape[1]):
        share = jnp.where(ids_ref[:, k : k + 1] == e, probs_ref[:, k : k + 1], share)
    return share


def pick_kernel(n, where_ref, ids_ref, *refs):
    pick_rows(n, where_ref[1], ids_ref, refs[:-1], refs[-1])


def pick(n, where, ids, hiddens, experts):
    inside = pl.BlockSpec(memory_space=pltpu.VMEM)
    return pl.pallas_call(
        functools.partial(pick_kernel, n),
        in_specs=[pl.BlockSpec(memory_space=pltpu.SMEM)] + [inside] * (1 + n),
        out_specs=inside,
        out_shape=jax.ShapeDtypeStruct((experts, ids.shape[0], hiddens[0].shape[2]), BF),
        compiler_params=pltpu.CompilerParams(vmem_limit_bytes=LIMIT),
        name="pick",
    )(where, ids, *hiddens)


def first_kernel(n, where_ref, ids_ref, probs_ref, *refs):
    hidden_refs, (wd_ref, out_ref, rows_ref) = refs[:n], refs[n:]
    pick_rows(n, where_ref[1], ids_ref, hidden_refs, rows_ref)
    half = out_ref.shape[2]
    tile = tile_of(half, 512)
    for e in range(wd_ref.shape[0]):
        share = share_of(ids_ref, probs_ref, e)
        for own in range(2):
            side = where_ref[0] if own else 1 - where_ref[0]
            for j in range(half // tile):
                columns = pl.ds(j * tile, tile)
                source = pl.ds(pl.multiple_of(side * half + j * tile, 128), tile)
                term = share * jnp.dot(rows_ref[e], wd_ref[e, :, source], preferred_element_type=F32)
                if e > 0:
                    term += out_ref[own, :, columns]
                out_ref[own, :, columns] = term


def first_down(n, where, ids, probs, hiddens, w_down):
    token_count = ids.shape[0]
    experts, _, width = w_down.shape
    depth = hiddens[0].shape[2]
    inside = pl.BlockSpec(memory_space=pltpu.VMEM)
    return pl.pallas_call(
        functools.partial(first_kernel, n),
        in_specs=[pl.BlockSpec(memory_space=pltpu.SMEM)] + [inside] * (3 + n),
        out_specs=inside,
        scratch_shapes=[pltpu.VMEM((experts, token_count, depth), BF)],
        out_shape=jax.ShapeDtypeStruct((2, token_count, width // 2), F32),
        cost_estimate=pl.CostEstimate(
            flops=2 * token_count * width * depth * experts,
            bytes_accessed=2 * experts * width * depth,
            transcendentals=0,
        ),
        compiler_params=pltpu.CompilerParams(vmem_limit_bytes=LIMIT),
        name="first_down",
    )(where, ids, probs, *hiddens, w_down)


def last_kernel(own, begin, where_ref, ids_ref, probs_ref, rows_ref, wd_ref, *refs):
    base_ref, (out_ref, acc_ref) = (refs[0] if len(refs) > 2 else None), refs[-2:]
    side = where_ref[0] if own else 1 - where_ref[0]
    experts, _, width = wd_ref.shape
    half = width // 2
    tile = tile_of(out_ref.shape[1], 256)
    for e in range(experts):
        share = share_of(ids_ref, probs_ref, e)
        for j in range(out_ref.shape[1] // tile):
            columns = pl.ds(j * tile, tile)
            source = pl.ds(pl.multiple_of(side * half + begin + j * tile, 128), tile)
            term = share * jnp.dot(rows_ref[e], wd_ref[e, :, source], preferred_element_type=F32)
            if e > 0:
                term += acc_ref[:, columns]
            elif base_ref is not None:
                term += base_ref[int(own), :, begin + j * tile : begin + (j + 1) * tile]
            if e < experts - 1:
                acc_ref[:, columns] = term
            else:
                out_ref[:, columns] = term


def last_down(where, ids, probs, rows, w_down, base, own, begin, end):
    token_count = ids.shape[0]
    experts, depth = w_down.shape[0], rows.shape[2]
    inside = pl.BlockSpec(memory_space=pltpu.VMEM)
    return pl.pallas_call(
        functools.partial(last_kernel, own, begin),
        in_specs=[pl.BlockSpec(memory_space=pltpu.SMEM)] + [inside] * (4 + len(base)),
        out_specs=inside,
        scratch_shapes=[pltpu.VMEM((token_count, end - begin), F32)],
        out_shape=jax.ShapeDtypeStruct((token_count, end - begin), F32),
        cost_estimate=pl.CostEstimate(
            flops=2 * token_count * (end - begin) * depth * experts,
            bytes_accessed=2 * experts * (end - begin) * depth,
            transcendentals=0,
        ),
        compiler_params=pltpu.CompilerParams(vmem_limit_bytes=LIMIT),
        name="down_own" if own else "down_other",
    )(where, ids, probs, rows, w_down, *base)


def sum_kernel(kept_ref, arrived_ref, out_ref):
    out_ref[...] = kept_ref[...] + arrived_ref[...].astype(F32)


def own_sum(kept, arrived):
    inside = pl.BlockSpec(memory_space=pltpu.VMEM)
    return pl.pallas_call(
        sum_kernel,
        in_specs=[inside] * 2,
        out_specs=inside,
        out_shape=jax.ShapeDtypeStruct(kept.shape, F32),
        compiler_params=pltpu.CompilerParams(vmem_limit_bytes=LIMIT),
        name="own_sum",
    )(kept, arrived)


def layer(tokens, route_ids, route_probs, w_gate, w_up, w_down):
    members = lax.axis_size("dp")
    n = lax.axis_size("tensor")
    lines = members // 4
    place = lax.axis_index("dp")
    side = place % 2
    me = lax.axis_index("tensor")
    where = jnp.stack([side, me, place // 2]).astype(jnp.int32)
    local_rows, width = tokens.shape
    half = width // 2
    first = side == 0
    experts, _, hidden_width = w_gate.shape
    w_gate = w_gate.reshape(experts, 2, half, hidden_width)
    w_up = w_up.reshape(experts, 2, half, hidden_width)
    chip_rows = 2 * local_rows
    parts = 2 if hidden_width % 256 == 0 else 1
    depth = hidden_width // parts
    cut = half // 128 * 2 // 3 * 128
    middle = (half // 128 + 1) // 2 * 128

    def flip(x, bits):
        return lax.ppermute(x, "dp", [(i, i ^ bits) for i in range(members)])

    def on_chip(x):
        return flip(x, 1)

    def over_x(x):
        return flip(x, 2)

    def over_z(x, k):
        return flip(x, 4 * k)

    def over_tensor(x):
        return [lax.ppermute(x[s - 1], "tensor", [(i, (i + s) % n) for i in range(n)]) for s in range(1, n)]

    def pair(mine, theirs, axis):
        return jnp.concatenate(
            [jnp.where(first, mine, theirs), jnp.where(first, theirs, mine)], axis=axis
        )

    def added(keep, arrived):
        for part in arrived:
            keep = keep + part.astype(F32)
        return keep

    left, right = tokens[:, :half], tokens[:, half:]
    theirs = on_chip(jnp.where(first, right, left))
    block = pair(jnp.where(first, left, right), theirs, 0)
    near, far = block[:, :cut], block[:, cut:]
    near_line = [near] + [over_z(near, k) for k in range(1, lines)]
    far_other = over_x(far)
    far_pair = [far, far_other]
    near_all = jnp.concatenate(near_line, axis=0)
    far_both = jnp.concatenate(far_pair, axis=0)
    near, w_up, where = lax.optimization_barrier((near, w_up, where))
    ids, probs, up_low = order(lines, chip_rows, where, route_ids, route_probs, w_up)
    near_all, far_both, w_gate, up_low = lax.optimization_barrier((near_all, far_both, w_gate, up_low))
    w_gate = fetch(w_gate.reshape(experts, 1, 2 * half, hidden_width), 0).reshape(experts, 2, half, hidden_width)
    near_other = over_x(near_all)
    far_line = [far_both] + [over_z(far_both, k) for k in range(1, lines)]
    near_other, far_line, w_gate = lax.optimization_barrier((near_other, far_line, w_gate))
    far_all = [jnp.concatenate([f[xr * chip_rows : (xr + 1) * chip_rows] for f in far_line], axis=0) for xr in range(2)]
    own = jnp.concatenate(
        [jnp.concatenate([near_all, near_other], axis=0), jnp.concatenate(far_all, axis=0)], axis=1
    )
    other = on_chip(own)

    base, up_high = gate_gemm(n, 0, where, ids, own, w_gate, w_up)
    keep_gate, send_gate = gate_gemm(n, 1, where, ids, other, w_gate, base)
    gate_arrived = over_tensor(send_gate)
    ups, up_arrived = [], []
    for part in range(parts):
        keep, send = up_gemm(n, part, parts, where, ids, own, other, [up_low, up_high])
        if part == parts - 1:
            send, w_down = lax.optimization_barrier((send, w_down))
            w_down = w_down.reshape(experts, parts, depth, width)
        ups.append(keep)
        up_arrived.append(over_tensor(send))
    down_parts, hiddens = [], []
    for part in range(parts):
        columns = slice(part * depth, (part + 1) * depth)
        if part > 0:
            w_down, hiddens[part - 1][0] = lax.optimization_barrier((w_down, hiddens[part - 1][0]))
        down_parts.append(fetch(w_down, part))
        up_arrived[part], down_parts[part] = lax.optimization_barrier((up_arrived[part], down_parts[part]))
        gate_sum = added(keep_gate[:, :, columns], [g[:, :, columns] for g in gate_arrived])
        up_sum = added(ups[part], up_arrived[part])
        hidden = (gate_sum * jax.nn.sigmoid(gate_sum) * up_sum).astype(BF)
        hiddens.append([hidden] + over_tensor([hidden] * (n - 1)))

    downs = []
    if parts > 1:
        downs = [first_down(n, where, ids, probs, hiddens[0], down_parts[0])]
    rows = pick(n, where, ids, hiddens[-1], experts)
    spans = ((0, middle), (middle, half))
    away = []
    for begin, end in spans:
        part = last_down(where, ids, probs, rows, down_parts[-1], downs, False, begin, end)
        part, rows = lax.optimization_barrier((part, rows))
        away.append(on_chip(part))
    kept, sent = [], []
    for i, (begin, end) in enumerate(spans):
        stay = last_down(where, ids, probs, rows, down_parts[-1], downs, True, begin, end)
        total = (stay + away[i]).reshape(2, lines, chip_rows, end - begin)
        part, rows = lax.optimization_barrier((total[1].astype(BF), rows))
        kept.append(total[0])
        sent.append(over_x(part))
    outs = []
    for i in range(len(spans)):
        line = kept[i] + sent[i].astype(F32)
        arrived = [over_z(line[k].astype(BF), k) for k in range(1, lines)]
        mine = own_sum(kept[i][0], sent[i][0])
        outs.append(added(mine, arrived))
    mixed = jnp.concatenate(outs, axis=1).astype(BF)
    upper, lower = mixed[:local_rows], mixed[local_rows:]
    others = on_chip(jnp.where(first, lower, upper))
    return pair(jnp.where(first, upper, lower), others, 1)


def solution(mesh):
    placed = (
        P("dp", "tensor"),
        P(),
        P(),
        P(None, "tensor", "dp"),
        P(None, "tensor", "dp"),
        P(None, "dp", "tensor"),
    )
    return jax.shard_map(layer, mesh=mesh, in_specs=placed, out_specs=P("dp", "tensor"), check_vma=False)
```

```python
import functools

import jax
import jax.numpy as jnp
from jax import lax
from jax.experimental import pallas as pl
from jax.experimental.pallas import tpu as pltpu
from jax.sharding import PartitionSpec as P


BF = jnp.bfloat16
F32 = jnp.float32
LIMIT = 10 * 1024 * 1024


def tile_of(width, most):
    tile = min(width, most)
    while width % tile:
        tile //= 2
    return tile


def copies_of(source, target, sem):
    count, depth = target.shape[0], target.shape[1] // 2
    copies = []
    for e in range(count):
        for part in range(2):
            piece = pl.ds(part * depth, depth)
            copies.append(pltpu.make_async_copy(source(e).at[piece], target.at[e, piece], sem.at[e, part]))
    return copies


def fetch_kernel(part, source_ref, target_ref, sem_ref):
    copies = copies_of(lambda e: source_ref.at[e, part], target_ref, sem_ref)
    for copy in copies:
        copy.start()
    for copy in copies:
        copy.wait()


def in_hbm(w):
    return pltpu.with_memory_space_constraint(w, pltpu.HBM)


def fetch(w, part):
    shape = w.shape[:1] + w.shape[2:]
    return pl.pallas_call(
        functools.partial(fetch_kernel, part),
        in_specs=[pl.BlockSpec(memory_space=pltpu.HBM)],
        out_specs=pl.BlockSpec(memory_space=pltpu.VMEM),
        out_shape=pltpu.VMEM(shape, w.dtype),
        scratch_shapes=[pltpu.SemaphoreType.DMA((w.shape[0], 2))],
        cost_estimate=pl.CostEstimate(flops=0, bytes_accessed=4 * w.size // w.shape[1], transcendentals=0),
        compiler_params=pltpu.CompilerParams(vmem_limit_bytes=LIMIT),
        name="fetch",
    )(in_hbm(w))


def order_kernel(lines, chip_rows, where_ref, ids_in, probs_in, wu_ref, ids_out, probs_out, fetched_ref, *scratch):
    ids_ref, probs_ref, sem_ref, small_sem = scratch
    small = [
        pltpu.make_async_copy(ids_in, ids_ref, small_sem.at[0]),
        pltpu.make_async_copy(probs_in, probs_ref, small_sem.at[1]),
    ]
    for copy in small:
        copy.start()
    copies = copies_of(lambda e: wu_ref.at[e], fetched_ref, sem_ref)
    for copy in copies:
        copy.start()
    for copy in small:
        copy.wait()
    top, token_count = ids_ref.shape
    row = lax.broadcasted_iota(jnp.int32, (chip_rows, token_count), 0)
    column = lax.broadcasted_iota(jnp.int32, (chip_rows, token_count), 1)
    for i, (xr, k) in enumerate((xr, k) for xr in range(2) for k in range(lines)):
        source = jnp.bitwise_xor(where_ref[2], 2 * k + xr) * chip_rows
        mine = column == row + source
        rows = slice(i * chip_rows, (i + 1) * chip_rows)
        for k in range(top):
            ids = jnp.where(mine, ids_ref[k : k + 1, :].astype(F32), 0.0)
            probs = jnp.where(mine, probs_ref[k : k + 1, :].astype(F32), 0.0)
            ids_out[rows, k : k + 1] = jnp.sum(ids, axis=1, keepdims=True).astype(jnp.int32)
            probs_out[rows, k : k + 1] = jnp.sum(probs, axis=1, keepdims=True)
    for copy in copies:
        copy.wait()


def order(lines, chip_rows, where, ids, probs, w_up):
    count = w_up.shape[0] - w_up.shape[0] // 2
    token_count, top = ids.shape
    inside = pl.BlockSpec(memory_space=pltpu.VMEM)
    return pl.pallas_call(
        functools.partial(order_kernel, lines, chip_rows),
        in_specs=[pl.BlockSpec(memory_space=pltpu.SMEM)] + [pl.BlockSpec(memory_space=pltpu.HBM)] * 3,
        out_specs=[inside] * 3,
        out_shape=[
            jax.ShapeDtypeStruct((token_count, top), jnp.int32),
            jax.ShapeDtypeStruct((token_count, top), F32),
            pltpu.VMEM((count,) + w_up.shape[1:], w_up.dtype),
        ],
        scratch_shapes=[
            pltpu.VMEM((top, token_count), jnp.int32),
            pltpu.VMEM((top, token_count), BF),
            pltpu.SemaphoreType.DMA((count, 2)),
            pltpu.SemaphoreType.DMA((2,)),
        ],
        cost_estimate=pl.CostEstimate(flops=0, bytes_accessed=4 * w_up.size // 2, transcendentals=0),
        compiler_params=pltpu.CompilerParams(vmem_limit_bytes=LIMIT),
        name="order",
    )(where, in_hbm(ids.T), in_hbm(probs.T), in_hbm(w_up))


def share_out(n, me, acc_ref, keep_ref, send_ref):
    rows = keep_ref.shape[1]
    for s in range(n):
        begin = pl.multiple_of(lax.rem(me + s, n) * rows, rows)
        block = acc_ref[:, pl.ds(begin, rows), :]
        if s == 0:
            keep_ref[...] = block
        else:
            send_ref[s - 1] = block.astype(BF)


def gate_kernel(n, stage, where_ref, ids_ref, rows_ref, wg_ref, *refs):
    copies = []
    if stage == 0:
        wu_ref, acc_ref, fetched_ref, sem_ref = refs
        last = wu_ref.shape[0] - fetched_ref.shape[0]
        copies = copies_of(lambda e: wu_ref.at[last + e], fetched_ref, sem_ref)
    else:
        base_ref, keep_ref, send_ref, acc_ref = refs
    for copy in copies:
        copy.start()
    half = where_ref[0] if stage == 0 else 1 - where_ref[0]
    tile = tile_of(wg_ref.shape[3], 256)
    for e in range(wg_ref.shape[0]):
        for j in range(wg_ref.shape[3] // tile):
            columns = pl.ds(j * tile, tile)
            block = jnp.dot(rows_ref[...], wg_ref[e, half, :, columns], preferred_element_type=F32)
            for k in range(acc_ref.shape[0]):
                value = block if stage == 0 else block + base_ref[k, :, columns]
                if e > 0:
                    value = jnp.where(ids_ref[:, k : k + 1] == e, value, acc_ref[k, :, columns])
                acc_ref[k, :, columns] = value
    if stage == 1:
        share_out(n, where_ref[1], acc_ref, keep_ref, send_ref)
    for copy in copies:
        copy.wait()


def gate_gemm(n, stage, where, ids, rows, w_gate, extra):
    token_count, top = ids.shape
    experts, _, half, hidden = w_gate.shape
    inside = pl.BlockSpec(memory_space=pltpu.VMEM)
    outside = pl.BlockSpec(memory_space=pltpu.HBM)
    whole = (top, token_count, hidden)
    count = experts // 2
    if stage == 0:
        extra, extra_spec = in_hbm(extra), outside
        out_shape = [jax.ShapeDtypeStruct(whole, F32), pltpu.VMEM((count, 2, half, hidden), BF)]
        scratch = [pltpu.SemaphoreType.DMA((count, 2))]
    else:
        extra_spec = inside
        out_shape = [
            jax.ShapeDtypeStruct((top, token_count // n, hidden), F32),
            jax.ShapeDtypeStruct((n - 1, top, token_count // n, hidden), BF),
        ]
        scratch = [pltpu.VMEM(whole, F32)]
    return pl.pallas_call(
        functools.partial(gate_kernel, n, stage),
        in_specs=[pl.BlockSpec(memory_space=pltpu.SMEM)] + [inside] * 3 + [extra_spec],
        out_specs=[inside] * len(out_shape),
        scratch_shapes=scratch,
        out_shape=out_shape,
        cost_estimate=pl.CostEstimate(
            flops=2 * token_count * half * hidden * experts,
            bytes_accessed=2 * experts * half * hidden,
            transcendentals=0,
        ),
        compiler_params=pltpu.CompilerParams(vmem_limit_bytes=LIMIT),
        name="gate_gemm",
    )(where, ids, rows, w_gate, extra)


def up_kernel(n, part, where_ref, ids_ref, own_ref, other_ref, *refs):
    weight_refs, (keep_ref, send_ref, acc_ref) = refs[:-3], refs[-3:]
    half = where_ref[0]
    tile = acc_ref.shape[2]
    columns = pl.ds(part * tile, tile)
    e = 0
    for w_ref in weight_refs:
        for i in range(w_ref.shape[0]):
            block = jnp.dot(own_ref[...], w_ref[i, half, :, columns], preferred_element_type=F32)
            block += jnp.dot(other_ref[...], w_ref[i, 1 - half, :, columns], preferred_element_type=F32)
            for k in range(acc_ref.shape[0]):
                value = block
                if e > 0:
                    value = jnp.where(ids_ref[:, k : k + 1] == e, value, acc_ref[k])
                acc_ref[k] = value
            e += 1
    share_out(n, where_ref[1], acc_ref, keep_ref, send_ref)


def up_gemm(n, part, parts, where, ids, own, other, weights):
    token_count, top = ids.shape
    half, hidden = weights[0].shape[2:]
    experts = sum(w.shape[0] for w in weights)
    rows = token_count // n
    tile = hidden // parts
    inside = pl.BlockSpec(memory_space=pltpu.VMEM)
    return pl.pallas_call(
        functools.partial(up_kernel, n, part),
        in_specs=[pl.BlockSpec(memory_space=pltpu.SMEM)] + [inside] * (3 + len(weights)),
        out_specs=[inside] * 2,
        scratch_shapes=[pltpu.VMEM((top, token_count, tile), F32)],
        out_shape=[
            jax.ShapeDtypeStruct((top, rows, tile), F32),
            jax.ShapeDtypeStruct((n - 1, top, rows, tile), BF),
        ],
        cost_estimate=pl.CostEstimate(
            flops=4 * token_count * half * tile * experts,
            bytes_accessed=4 * experts * half * tile,
            transcendentals=0,
        ),
        compiler_params=pltpu.CompilerParams(vmem_limit_bytes=LIMIT),
        name="up_gemm",
    )(where, ids, own, other, *weights)


def pick_rows(n, me, ids_ref, hidden_refs, rows_ref):
    top, rows, depth = hidden_refs[0].shape
    for s in range(n):
        begin = pl.multiple_of(lax.rem(me + n - s, n) * rows, rows)
        for e in range(rows_ref.shape[0]):
            total = jnp.zeros((rows, depth), F32)
            for k in range(top):
                chosen = ids_ref[pl.ds(begin, rows), k : k + 1] == e
                total = jnp.where(chosen, hidden_refs[s][k].astype(F32), total)
            rows_ref[e, pl.ds(begin, rows), :] = total.astype(BF)


def share_of(ids_ref, probs_ref, e):
    share = jnp.zeros((ids_ref.shape[0], 1), F32)
    for k in range(ids_ref.shape[1]):
        share = jnp.where(ids_ref[:, k : k + 1] == e, probs_ref[:, k : k + 1], share)
    return share


def pick_kernel(n, where_ref, ids_ref, *refs):
    pick_rows(n, where_ref[1], ids_ref, refs[:-1], refs[-1])


def pick(n, where, ids, hiddens, experts):
    inside = pl.BlockSpec(memory_space=pltpu.VMEM)
    return pl.pallas_call(
        functools.partial(pick_kernel, n),
        in_specs=[pl.BlockSpec(memory_space=pltpu.SMEM)] + [inside] * (1 + n),
        out_specs=inside,
        out_shape=jax.ShapeDtypeStruct((experts, ids.shape[0], hiddens[0].shape[2]), BF),
        compiler_params=pltpu.CompilerParams(vmem_limit_bytes=LIMIT),
        name="pick",
    )(where, ids, *hiddens)


def first_kernel(n, where_ref, ids_ref, probs_ref, *refs):
    hidden_refs, (wd_ref, out_ref, rows_ref) = refs[:n], refs[n:]
    pick_rows(n, where_ref[1], ids_ref, hidden_refs, rows_ref)
    half = out_ref.shape[2]
    tile = tile_of(half, 512)
    for e in range(wd_ref.shape[0]):
        share = share_of(ids_ref, probs_ref, e)
        for own in range(2):
            side = where_ref[0] if own else 1 - where_ref[0]
            for j in range(half // tile):
                columns = pl.ds(j * tile, tile)
                source = pl.ds(pl.multiple_of(side * half + j * tile, 128), tile)
                term = share * jnp.dot(rows_ref[e], wd_ref[e, :, source], preferred_element_type=F32)
                if e > 0:
                    term += out_ref[own, :, columns]
                out_ref[own, :, columns] = term


def first_down(n, where, ids, probs, hiddens, w_down):
    token_count = ids.shape[0]
    experts, _, width = w_down.shape
    depth = hiddens[0].shape[2]
    inside = pl.BlockSpec(memory_space=pltpu.VMEM)
    return pl.pallas_call(
        functools.partial(first_kernel, n),
        in_specs=[pl.BlockSpec(memory_space=pltpu.SMEM)] + [inside] * (3 + n),
        out_specs=inside,
        scratch_shapes=[pltpu.VMEM((experts, token_count, depth), BF)],
        out_shape=jax.ShapeDtypeStruct((2, token_count, width // 2), F32),
        cost_estimate=pl.CostEstimate(
            flops=2 * token_count * width * depth * experts,
            bytes_accessed=2 * experts * width * depth,
            transcendentals=0,
        ),
        compiler_params=pltpu.CompilerParams(vmem_limit_bytes=LIMIT),
        name="first_down",
    )(where, ids, probs, *hiddens, w_down)


def last_kernel(own, begin, where_ref, ids_ref, probs_ref, rows_ref, wd_ref, *refs):
    base_ref, (out_ref, acc_ref) = (refs[0] if len(refs) > 2 else None), refs[-2:]
    side = where_ref[0] if own else 1 - where_ref[0]
    experts, _, width = wd_ref.shape
    half = width // 2
    tile = tile_of(out_ref.shape[1], 256)
    for e in range(experts):
        share = share_of(ids_ref, probs_ref, e)
        for j in range(out_ref.shape[1] // tile):
            columns = pl.ds(j * tile, tile)
            source = pl.ds(pl.multiple_of(side * half + begin + j * tile, 128), tile)
            term = share * jnp.dot(rows_ref[e], wd_ref[e, :, source], preferred_element_type=F32)
            if e > 0:
                term += acc_ref[:, columns]
            elif base_ref is not None:
                term += base_ref[int(own), :, begin + j * tile : begin + (j + 1) * tile]
            if e < experts - 1:
                acc_ref[:, columns] = term
            else:
                out_ref[:, columns] = term


def last_down(where, ids, probs, rows, w_down, base, own, begin, end):
    token_count = ids.shape[0]
    experts, depth = w_down.shape[0], rows.shape[2]
    inside = pl.BlockSpec(memory_space=pltpu.VMEM)
    return pl.pallas_call(
        functools.partial(last_kernel, own, begin),
        in_specs=[pl.BlockSpec(memory_space=pltpu.SMEM)] + [inside] * (4 + len(base)),
        out_specs=inside,
        scratch_shapes=[pltpu.VMEM((token_count, end - begin), F32)],
        out_shape=jax.ShapeDtypeStruct((token_count, end - begin), F32),
        cost_estimate=pl.CostEstimate(
            flops=2 * token_count * (end - begin) * depth * experts,
            bytes_accessed=2 * experts * (end - begin) * depth,
            transcendentals=0,
        ),
        compiler_params=pltpu.CompilerParams(vmem_limit_bytes=LIMIT),
        name="down_own" if own else "down_other",
    )(where, ids, probs, rows, w_down, *base)


def sum_kernel(kept_ref, arrived_ref, out_ref):
    out_ref[...] = kept_ref[...] + arrived_ref[...].astype(F32)


def own_sum(kept, arrived):
    inside = pl.BlockSpec(memory_space=pltpu.VMEM)
    return pl.pallas_call(
        sum_kernel,
        in_specs=[inside] * 2,
        out_specs=inside,
        out_shape=jax.ShapeDtypeStruct(kept.shape, F32),
        compiler_params=pltpu.CompilerParams(vmem_limit_bytes=LIMIT),
        name="own_sum",
    )(kept, arrived)


def layer(tokens, route_ids, route_probs, w_gate, w_up, w_down):
    members = lax.axis_size("dp")
    n = lax.axis_size("tensor")
    lines = members // 4
    place = lax.axis_index("dp")
    side = place % 2
    me = lax.axis_index("tensor")
    where = jnp.stack([side, me, place // 2]).astype(jnp.int32)
    local_rows, width = tokens.shape
    half = width // 2
    first = side == 0
    experts, _, hidden_width = w_gate.shape
    w_gate = w_gate.reshape(experts, 2, half, hidden_width)
    w_up = w_up.reshape(experts, 2, half, hidden_width)
    chip_rows = 2 * local_rows
    parts = 2 if hidden_width % 256 == 0 else 1
    depth = hidden_width // parts
    cut = half // 128 * 2 // 3 * 128
    middle = (half // 128 + 1) // 2 * 128

    def flip(x, bits):
        return lax.ppermute(x, "dp", [(i, i ^ bits) for i in range(members)])

    def on_chip(x):
        return flip(x, 1)

    def over_x(x):
        return flip(x, 2)

    def over_z(x, k):
        return flip(x, 4 * k)

    def over_tensor(x):
        return [lax.ppermute(x[s - 1], "tensor", [(i, (i + s) % n) for i in range(n)]) for s in range(1, n)]

    def pair(mine, theirs, axis):
        return jnp.concatenate(
            [jnp.where(first, mine, theirs), jnp.where(first, theirs, mine)], axis=axis
        )

    def added(keep, arrived):
        for part in arrived:
            keep = keep + part.astype(F32)
        return keep

    theirs = on_chip(tokens)
    upper = jnp.where(first, tokens[:, :half], theirs[:, half:])
    lower = jnp.where(first, theirs[:, :half], tokens[:, half:])
    block = jnp.concatenate([upper, lower], axis=0)
    near, far = block[:, :cut], block[:, cut:]
    near_line = [near] + [over_z(near, k) for k in range(1, lines)]
    far_other = over_x(far)
    far_pair = [far, far_other]
    near_all = jnp.concatenate(near_line, axis=0)
    far_both = jnp.concatenate(far_pair, axis=0)
    near, w_up, where = lax.optimization_barrier((near, w_up, where))
    ids, probs, up_low = order(lines, chip_rows, where, route_ids, route_probs, w_up)
    near_all, far_both, w_gate, up_low = lax.optimization_barrier((near_all, far_both, w_gate, up_low))
    w_gate = fetch(w_gate.reshape(experts, 1, 2 * half, hidden_width), 0).reshape(experts, 2, half, hidden_width)
    near_other = over_x(near_all)
    far_line = [far_both] + [over_z(far_both, k) for k in range(1, lines)]
    near_other, far_line, w_gate = lax.optimization_barrier((near_other, far_line, w_gate))
    far_all = [jnp.concatenate([f[xr * chip_rows : (xr + 1) * chip_rows] for f in far_line], axis=0) for xr in range(2)]
    own = jnp.concatenate(
        [jnp.concatenate([near_all, near_other], axis=0), jnp.concatenate(far_all, axis=0)], axis=1
    )
    other = on_chip(own)

    base, up_high = gate_gemm(n, 0, where, ids, own, w_gate, w_up)
    keep_gate, send_gate = gate_gemm(n, 1, where, ids, other, w_gate, base)
    gate_arrived = over_tensor(send_gate)
    ups, up_arrived = [], []
    for part in range(parts):
        keep, send = up_gemm(n, part, parts, where, ids, own, other, [up_low, up_high])
        if part == parts - 1:
            send, w_down = lax.optimization_barrier((send, w_down))
            w_down = w_down.reshape(experts, parts, depth, width)
        ups.append(keep)
        up_arrived.append(over_tensor(send))
    down_parts, hiddens = [], []
    for part in range(parts):
        columns = slice(part * depth, (part + 1) * depth)
        if part > 0:
            w_down, hiddens[part - 1][0] = lax.optimization_barrier((w_down, hiddens[part - 1][0]))
        down_parts.append(fetch(w_down, part))
        up_arrived[part], down_parts[part] = lax.optimization_barrier((up_arrived[part], down_parts[part]))
        gate_sum = added(keep_gate[:, :, columns], [g[:, :, columns] for g in gate_arrived])
        up_sum = added(ups[part], up_arrived[part])
        hidden = (gate_sum * jax.nn.sigmoid(gate_sum) * up_sum).astype(BF)
        hiddens.append([hidden] + over_tensor([hidden] * (n - 1)))

    downs = []
    if parts > 1:
        downs = [first_down(n, where, ids, probs, hiddens[0], down_parts[0])]
    rows = pick(n, where, ids, hiddens[-1], experts)
    spans = ((0, middle), (middle, half))
    kept, sent = [], []
    for begin, end in spans:
        shape = (2, lines, chip_rows, end - begin)
        away = on_chip(last_down(where, ids, probs, rows, down_parts[-1], downs, False, begin, end))
        stay = last_down(where, ids, probs, rows, down_parts[-1], downs, True, begin, end)
        away, stay = away.reshape(shape), stay.reshape(shape)
        part, rows = lax.optimization_barrier(((stay[1] + away[1]).astype(BF), rows))
        sent.append(over_x(part))
        kept.append(own_sum(stay[0], away[0]))
    outs = []
    for i in range(len(spans)):
        line = kept[i][1:] + sent[i][1:].astype(F32)
        arrived = [over_z(line[k - 1].astype(BF), k) for k in range(1, lines)]
        mine = own_sum(kept[i][0], sent[i][0])
        outs.append(added(mine, arrived))
    mixed = jnp.concatenate(outs, axis=1).astype(BF)
    upper, lower = mixed[:local_rows], mixed[local_rows:]
    others = on_chip(jnp.where(first, lower, upper))
    return pair(jnp.where(first, upper, lower), others, 1)


def solution(mesh):
    placed = (
        P("dp", "tensor"),
        P(),
        P(),
        P(None, "tensor", "dp"),
        P(None, "tensor", "dp"),
        P(None, "dp", "tensor"),
    )
    return jax.shard_map(layer, mesh=mesh, in_specs=placed, out_specs=P("dp", "tensor"), check_vma=False)
```
